32 devices in a mesh: phi: 4 (over y, x), theta: 8 (over z, core).
Axes of the slice: x: 2, y: 2, z: 4, core: 2. Of those that a mesh axis runs over, the one named last changes fastest.
Arguments:
- subtree_pattern: bfloat16 [256, 2, 32, 64, 128], P(('phi', 'theta')), may hold values from -6 to 6
- up_phi: bfloat16 [128, 256], replicated, may hold values from -0.5 to 0.5
- up_theta: bfloat16 [128, 64], replicated, may hold values from -0.75 to 0.75
- offsets: float32 [3, 256], P(None, ('phi', 'theta')), may hold values from -8 to 8
- theta_start: int32 [256], P('theta'), may hold values from -2 to 126, as said below
- theta_frac: float32 [256], P('theta'), may hold values from 0 to 1
- phi_start: int32 [1024], P('phi'), may hold values from -2 to 254, as said below
- phi_frac: float32 [1024], P('phi'), may hold values from 0 to 1
Outputs:
- rcs: float32 [16, 256, 1024], P(None, 'theta', 'phi')
The draws below stay inside these ranges and needn't reach their ends.
Inputs may be any that keep to these rules, and one draw needn't show every extreme that they name: `theta_start`: row o lies in polar band b = o // 32; its start is b * (128 // 8) + k with k from -2 to 128 // 8 - 2; the first row of each band has k = -2 and the last k = 128 // 8 - 2. `phi_start`: column w lies in azimuth band b = w // 256; its start is b * (256 // 4) + k with k from -2 to 256 // 4 - 2, read periodically; the first column of each band has k = -2 and the last k = 256 // 4 - 2.
All inputs are finite; a program needn't handle non-finite values.
Results may differ from the reference program's by a relative error of at most 0.0024.
Values sent between devices are 32-bit elements; how exact they have to be, the bound alone decides.
A program may use at most 128 MiB of HBM per device.

```python
import math
import jax
import jax.numpy as jnp
from jax import lax

NT = 128
NP = 256
MT = 64
MP = 128
INC = 16
OT_DEV = 32
OP_DEV = 256
QUANT = 32
SUBTREES = 256
NOT = 256
NOP = 1024
N_PHI = 4
N_THETA = 8


def band_starts(key, total_rows, rows_band, nodes_band):
    rows = jnp.arange(total_rows, dtype=jnp.int32)
    band = rows // rows_band
    within = rows % rows_band
    drawn = jax.random.randint(jax.random.fold_in(key, 7), (total_rows,), -2, nodes_band - 1)
    drawn = jnp.where(within == 0, -2, jnp.where(within == rows_band - 1, nodes_band - 2, drawn))
    return (band * nodes_band + drawn).astype(jnp.int32)


def draw_theta_start(key, part):
    return band_starts(key, NOT, OT_DEV, NT // N_THETA)


def draw_phi_start(key, part):
    return band_starts(key, NOP, OP_DEV, NP // N_PHI)


def level_of(own_key, extent, pieces, smallest, top_value):
    factor_of = 1.0
    for axis_at, shards_of in pieces:
        heights = jax.random.uniform(jax.random.fold_in(jax.random.fold_in(own_key, 6), axis_at), (shards_of,), jnp.float32, smallest / len(pieces), top_value / len(pieces))
        factor_of = factor_of * jnp.repeat(jnp.exp(heights), extent[axis_at] // shards_of).reshape((-1,) + (1,) * (len(extent) - 1 - axis_at))
    return factor_of


def gaussian(stream_key, shape, deviation, most, split=(), kind=jnp.bfloat16):
    gain = level_of(stream_key, shape, split, -0.22, 0.18) if split else 1.0
    values = jax.random.normal(stream_key, shape, jnp.float32) * deviation * gain
    return jnp.minimum(jnp.maximum(values, -most), most).astype(kind)


def setup_inputs(seed: int = 0) -> dict:
    splits = jax.random.split(jax.random.key(seed), 9)
    subtree_pattern = gaussian(splits[0], (SUBTREES, 2, QUANT, MT, MP), 1.0, 6.0, ((0, 32),))
    up_phi = gaussian(splits[1], (MP, NP), MP ** -0.5, 0.5)
    up_theta = gaussian(splits[2], (NT, MT), MT ** -0.5, 0.75)
    offsets = jnp.clip(jax.random.uniform(splits[3], (3, SUBTREES), jnp.float32, -8.0, 8.0) * level_of(splits[3], (3, SUBTREES), ((1, 32),), -0.4, 0.0), -8.0, 8.0)
    theta_start = draw_theta_start(jax.random.fold_in(splits[8], 71), 0)
    theta_frac = jnp.clip(1.0 * jax.random.uniform(splits[5], (NOT,), jnp.float32) ** level_of(splits[5], (NOT,), ((0, 8),), -0.2, 0.2), 0.0, 1.0)
    phi_start = draw_phi_start(jax.random.fold_in(splits[8], 71), 0)
    phi_frac = jnp.clip(1.0 * jax.random.uniform(splits[7], (NOP,), jnp.float32) ** level_of(splits[7], (NOP,), ((0, 4),), -0.2, 0.2), 0.0, 1.0)
    return {"subtree_pattern": subtree_pattern, "up_phi": up_phi, "up_theta": up_theta, "offsets": offsets, "theta_start": theta_start, "theta_frac": theta_frac, "phi_start": phi_start, "phi_frac": phi_frac}


def directions():
    polar = (jnp.arange(NT, dtype=jnp.float32) + 0.5) * (math.pi / NT)
    azimuth = jnp.arange(NP, dtype=jnp.float32) * (2.0 * math.pi / NP)
    sine_polar = jnp.sin(polar)[:, None]
    unit_x = sine_polar * jnp.cos(azimuth)[None, :]
    unit_y = sine_polar * jnp.sin(azimuth)[None, :]
    unit_z = jnp.cos(polar)[:, None] * jnp.ones((1, NP), jnp.float32)
    return unit_x, unit_y, unit_z


def shift_centre(fine_grid, offset, unit_x, unit_y, unit_z):
    phase_angle = (2.0 * math.pi) * (offset[0] * unit_x + offset[1] * unit_y + offset[2] * unit_z)
    cosine = jnp.cos(phase_angle)
    sine_part = jnp.sin(phase_angle)
    real_part = fine_grid[0] * cosine - fine_grid[1] * sine_part
    imag_part = fine_grid[0] * sine_part + fine_grid[1] * cosine
    return jnp.stack([real_part, imag_part])


def lagrange_matrix(start, frac, width):
    position = 1.0 + frac
    weights = [-(position - 1.0) * (position - 2.0) * (position - 3.0) / 6.0,
               position * (position - 2.0) * (position - 3.0) / 2.0,
               -position * (position - 1.0) * (position - 3.0) / 2.0,
               position * (position - 1.0) * (position - 2.0) / 6.0]
    columns = jnp.arange(width, dtype=jnp.int32)[None, :]
    matrix = jnp.zeros((start.shape[0], width), frac.dtype)
    for tap in range(4):
        matrix = matrix + jnp.where(columns == (start + tap)[:, None], weights[tap][:, None], 0.0)
    return matrix


def reference(subtree_pattern, up_phi, up_theta, offsets, theta_start, theta_frac, phi_start, phi_frac):
    unit_x, unit_y, unit_z = directions()
    phi_matrix = up_phi.astype(jnp.float32)
    theta_matrix = up_theta.astype(jnp.float32)

    def add_subtree(total, inputs):
        pattern, offset = inputs
        coarse = jnp.einsum('rqmp,pn->rqmn', pattern.astype(jnp.float32), phi_matrix).astype(jnp.bfloat16)
        coarse = lax.optimization_barrier(coarse)
        fine_grid = jnp.einsum('tm,rqmn->rqtn', theta_matrix, coarse.astype(jnp.float32))
        return total + shift_centre(fine_grid, offset, unit_x, unit_y, unit_z), None

    zeros = jnp.zeros((2, QUANT, NT, NP), jnp.float32)
    root, ignored = lax.scan(add_subtree, zeros, (subtree_pattern, offsets.T))
    padded = jnp.pad(root, ((0, 0), (0, 0), (2, 2), (0, 0)))
    padded = jnp.concatenate([padded[..., NP - 2:], padded, padded[..., :2]], axis=3)
    theta_weights = lagrange_matrix(theta_start + 2, theta_frac, NT + 4)
    phi_weights = lagrange_matrix(phi_start + 2, phi_frac, NP + 4)
    field = jnp.einsum('ot,rqtp->rqop', theta_weights, padded, precision=lax.Precision.HIGHEST)
    field = jnp.einsum('rqop,wp->rqow', field, phi_weights, precision=lax.Precision.HIGHEST)
    power = (field * field).reshape(4, INC, NOT, NOP)
    return jnp.sum(power, axis=0) / SUBTREES
```

```python
import functools
import math

import jax
import jax.numpy as jnp
import numpy as np
from jax import lax
from jax.experimental import pallas as pl
from jax.experimental.pallas import tpu as pltpu
from jax.sharding import PartitionSpec as P

NT = 128
NP = 256
LANES = 128


def padded_2(block, sides, width, periodic):
    for axis, dim in sides:
        count = lax.axis_size(axis)
        forward = [(i, i + 1) for i in range(count - 1)]
        if periodic:
            forward.append((count - 1, 0))
        backward = [(target, source) for source, target in forward]
        low = lax.ppermute(
            lax.slice_in_dim(block, block.shape[dim] - width, None, axis=dim), axis, forward
        )
        high = lax.ppermute(lax.slice_in_dim(block, 0, width, axis=dim), axis, backward)
        block = jnp.concatenate([low, block, high], axis=dim)
    return block


def direction_tables(group, bands):
    polar = (np.arange(NT) + 0.5) * (math.pi / NT)
    rows = np.stack([np.sin(polar), np.cos(polar)])[:, :, None]
    rows = np.broadcast_to(rows, (2, NT, LANES))
    azimuth = (np.arange(NP) * (2.0 * math.pi / NP)).reshape(bands, 1, -1)
    azimuth = np.broadcast_to(azimuth, (bands, group, azimuth.shape[2])).reshape(1, -1)
    columns = np.stack([np.cos(azimuth), np.sin(azimuth)])
    columns = np.broadcast_to(columns, (2, 8, columns.shape[2]))
    return rows.astype(np.float32), columns.astype(np.float32)


def grouped_up_phi(up_phi, group, bands):
    split = up_phi.reshape(up_phi.shape[0], bands, 1, NP // bands)
    blocks = []
    for g in range(group):
        pads = [(0, 0), (0, 0), (g, group - 1 - g), (0, 0)]
        blocks.append(jnp.pad(split, pads).reshape(up_phi.shape[0], -1))
    return jnp.concatenate(blocks, axis=0)


def turn_series():
    two_pi = 2.0 * math.pi
    sine = [(-1) ** k * two_pi ** (2 * k + 1) / math.factorial(2 * k + 1) for k in range(9)]
    cosine = [(-1) ** k * two_pi ** (2 * k) / math.factorial(2 * k) for k in range(10)]
    return sine, cosine


def horner(square, terms):
    value = jnp.full_like(square, terms[-1])
    for term in terms[-2::-1]:
        value = value * square + term
    return value


def phase_factors(offsets_ref, row_ref, column_ref, cos_ref, sin_ref):
    sine_terms, cosine_terms = turn_series()
    lane_groups = cos_ref.shape[2] // LANES

    @pl.loop(0, cos_ref.shape[0])
    def _(s):
        off_x, off_y, off_z = (offsets_ref[k, s] for k in range(3))
        for lane in range(lane_groups):
            lanes = slice(lane * LANES, (lane + 1) * LANES)
            wave = off_x * column_ref[0, 0:1, lanes] + off_y * column_ref[1, 0:1, lanes]
            turns = wave * row_ref[0] + off_z * row_ref[1]
            turns = turns - jnp.floor(turns + 0.5)
            square = turns * turns
            cos_ref[s, :, lanes] = horner(square, cosine_terms)
            sin_ref[s, :, lanes] = horner(square, sine_terms) * turns


def subtree_sum(i, pattern_ref, phi_ref, theta_ref, coarse_ref, cos_ref, sin_ref, store):
    count, parts, group, _, polar, _ = pattern_ref.shape
    rows = [
        jnp.concatenate([pattern_ref[s, r, g, i] for g in range(group)], axis=1)
        for s in range(count)
        for r in range(parts)
    ]
    coarse_ref[...] = jnp.dot(
        jnp.concatenate(rows, axis=0), phi_ref[...], preferred_element_type=jnp.float32
    ).astype(jnp.bfloat16)
    width = 2 * LANES
    for start in range(0, phi_ref.shape[1], width):
        lanes = slice(start, start + width)
        real_sum, imag_sum = None, None
        for s in range(count):
            real, imag = (
                jnp.dot(
                    theta_ref[...],
                    coarse_ref[(s * parts + r) * polar : (s * parts + r + 1) * polar, lanes],
                    preferred_element_type=jnp.float32,
                )
                for r in range(parts)
            )
            cosine, sine = cos_ref[s, :, lanes], sin_ref[s, :, lanes]
            real_part = real * cosine - imag * sine
            imag_part = real * sine + imag * cosine
            real_sum = real_part if s == 0 else real_sum + real_part
            imag_sum = imag_part if s == 0 else imag_sum + imag_part
        for k in range(width // LANES):
            piece = slice(k * LANES, (k + 1) * LANES)
            store(start // LANES + k, 0, real_sum[:, piece])
            store(start // LANES + k, 1, imag_sum[:, piece])


def sum_kernel(
    pattern_ref, phi_ref, theta_ref, offsets_ref, row_ref, column_ref, out_ref,
    cos_ref, sin_ref, coarse_ref,
):
    phase_factors(offsets_ref, row_ref, column_ref, cos_ref, sin_ref)
    bands_theta, _, _, units, band_theta, _ = out_ref.shape

    @pl.loop(0, units)
    def _(i):
        def store(band, part, value):
            out_ref[:, band, part, i] = value.reshape(bands_theta, band_theta, LANES)

        subtree_sum(i, pattern_ref, phi_ref, theta_ref, coarse_ref, cos_ref, sin_ref, store)


def lagrange_matrix(start, frac, width):
    position = 1.0 + frac
    weights = [
        -(position - 1.0) * (position - 2.0) * (position - 3.0) / 6.0,
        position * (position - 2.0) * (position - 3.0) / 2.0,
        -position * (position - 1.0) * (position - 3.0) / 2.0,
        position * (position - 1.0) * (position - 2.0) / 6.0,
    ]
    columns = jnp.arange(width, dtype=jnp.int32)[None, :]
    matrix = jnp.zeros((start.shape[0], width), jnp.float32)
    for tap in range(4):
        matrix = matrix + jnp.where(columns == (start + tap)[:, None], weights[tap][:, None], 0.0)
    return matrix


def per_device(
    subtree_pattern, up_phi, up_theta, offsets, theta_start, theta_frac, phi_start, phi_frac
):
    count_phi = lax.axis_size("phi")
    count_theta = lax.axis_size("theta")
    band_theta = NT // count_theta
    band_phi = NP // count_phi
    group = LANES // band_phi
    held, parts, channels, polar, azimuth = subtree_pattern.shape
    units = channels // group
    pattern = subtree_pattern.reshape(held, parts, group, units, polar, azimuth)
    up_phi_grouped = grouped_up_phi(up_phi, group, count_phi)
    rows, columns = direction_tables(group, count_phi)
    whole = pl.BlockSpec(memory_space=pltpu.VMEM)
    total = pl.pallas_call(
        sum_kernel,
        out_shape=jax.ShapeDtypeStruct(
            (count_theta, count_phi, parts, units, band_theta, LANES), jnp.float32
        ),
        in_specs=[whole, whole, whole, pl.BlockSpec(memory_space=pltpu.SMEM), whole, whole],
        out_specs=whole,
        scratch_shapes=[
            pltpu.VMEM((held, NT, count_phi * LANES), jnp.float32),
            pltpu.VMEM((held, NT, count_phi * LANES), jnp.float32),
            pltpu.VMEM((held * parts * polar, count_phi * LANES), jnp.bfloat16),
        ],
        compiler_params=pltpu.CompilerParams(vmem_limit_bytes=56 << 20),
    )(pattern, up_phi_grouped, up_theta, offsets, jnp.asarray(rows), jnp.asarray(columns))
    partial_band = lax.psum_scatter(total, "theta", scatter_dimension=0, tiled=False)
    root = lax.psum_scatter(partial_band, "phi", scatter_dimension=0, tiled=False)
    root = root.reshape(parts, units, band_theta, group, band_phi)
    root = root.transpose(0, 3, 1, 2, 4).reshape(parts, channels, band_theta, band_phi)
    padded = padded_2(root, (("theta", 2),), 2, False)
    padded = padded_2(padded, (("phi", 3),), 2, True)
    local_theta = theta_start - lax.axis_index("theta") * band_theta + 2
    local_phi = phi_start - lax.axis_index("phi") * band_phi + 2
    theta_weights = lagrange_matrix(local_theta, theta_frac, band_theta + 4)
    phi_weights = lagrange_matrix(local_phi, phi_frac, band_phi + 4)
    field = jnp.einsum("ot,rqtp->rqop", theta_weights, padded, precision=lax.Precision.HIGHEST)
    field = jnp.einsum("rqop,wp->rqow", field, phi_weights, precision=lax.Precision.HIGHEST)
    subtrees = held * count_phi * count_theta
    power = (field * field).reshape(4, channels // 2, field.shape[2], field.shape[3])
    return jnp.sum(power, axis=0) / subtrees


def solution(mesh):
    return jax.shard_map(
        per_device,
        mesh=mesh,
        in_specs=(
            P(("phi", "theta"), None, None, None, None),
            P(),
            P(),
            P(None, ("phi", "theta")),
            P("theta"),
            P("theta"),
            P("phi"),
            P("phi"),
        ),
        out_specs=P(None, "theta", "phi"),
        check_vma=False,
    )
```

```python
import math

import jax
import jax.numpy as jnp
import numpy as np
from jax import lax
from jax.experimental import pallas as pl
from jax.experimental.pallas import tpu as pltpu
from jax.sharding import PartitionSpec as P

NT = 128
NP = 256
LANES = 128
CHUNKS = 8
FIRST_LAG = 3
SECOND_LAG = 5


def padded_2(block, sides, width, periodic):
    for axis, dim in sides:
        count = lax.axis_size(axis)
        forward = [(i, i + 1) for i in range(count - 1)]
        if periodic:
            forward.append((count - 1, 0))
        backward = [(target, source) for source, target in forward]
        low = lax.ppermute(
            lax.slice_in_dim(block, block.shape[dim] - width, None, axis=dim), axis, forward
        )
        high = lax.ppermute(lax.slice_in_dim(block, 0, width, axis=dim), axis, backward)
        block = jnp.concatenate([low, block, high], axis=dim)
    return block


def direction_tables(group, bands):
    polar = (np.arange(NT) + 0.5) * (math.pi / NT)
    rows = np.stack([np.sin(polar), np.cos(polar)])[:, :, None]
    rows = np.broadcast_to(rows, (2, NT, LANES))
    azimuth = (np.arange(NP) * (2.0 * math.pi / NP)).reshape(bands, 1, -1)
    azimuth = np.broadcast_to(azimuth, (bands, group, azimuth.shape[2])).reshape(1, -1)
    columns = np.stack([np.cos(azimuth), np.sin(azimuth)])
    columns = np.broadcast_to(columns, (2, 8, columns.shape[2]))
    return rows.astype(np.float32), columns.astype(np.float32)


def grouped_up_phi(up_phi, group, bands):
    split = up_phi.reshape(up_phi.shape[0], bands, 1, NP // bands)
    blocks = []
    for g in range(group):
        pads = [(0, 0), (0, 0), (g, group - 1 - g), (0, 0)]
        blocks.append(jnp.pad(split, pads).reshape(up_phi.shape[0], -1))
    return jnp.concatenate(blocks, axis=0)


def turn_series():
    two_pi = 2.0 * math.pi
    sine = [(-1) ** k * two_pi ** (2 * k + 1) / math.factorial(2 * k + 1) for k in range(9)]
    cosine = [(-1) ** k * two_pi ** (2 * k) / math.factorial(2 * k) for k in range(10)]
    return sine, cosine


def horner(square, terms):
    value = jnp.full_like(square, terms[-1])
    for term in terms[-2::-1]:
        value = value * square + term
    return value


def phase_factors(offsets_ref, row_ref, column_ref, cos_ref, sin_ref):
    sine_terms, cosine_terms = turn_series()
    lane_groups = cos_ref.shape[2] // LANES

    @pl.loop(0, cos_ref.shape[0])
    def _(s):
        off_x, off_y, off_z = (offsets_ref[k, s] for k in range(3))
        for lane in range(lane_groups):
            lanes = slice(lane * LANES, (lane + 1) * LANES)
            wave = off_x * column_ref[0, 0:1, lanes] + off_y * column_ref[1, 0:1, lanes]
            turns = wave * row_ref[0] + off_z * row_ref[1]
            turns = turns - jnp.floor(turns + 0.5)
            square = turns * turns
            cos_ref[s, :, lanes] = horner(square, cosine_terms)
            sin_ref[s, :, lanes] = horner(square, sine_terms) * turns


def subtree_sum(pattern, phi_ref, theta_ref, coarse_ref, cos_ref, sin_ref, store):
    count, polar = cos_ref.shape[0], theta_ref.shape[1]
    parts = coarse_ref.shape[0] // (count * polar)
    rows = [pattern(s, r) for s in range(count) for r in range(parts)]
    coarse_ref[...] = jnp.dot(
        jnp.concatenate(rows, axis=0), phi_ref[...], preferred_element_type=jnp.float32
    ).astype(jnp.bfloat16)
    width = 2 * LANES
    for start in range(0, phi_ref.shape[1], width):
        lanes = slice(start, start + width)
        real_sum, imag_sum = None, None
        for s in range(count):
            real, imag = (
                jnp.dot(
                    theta_ref[...],
                    coarse_ref[(s * parts + r) * polar : (s * parts + r + 1) * polar, lanes],
                    preferred_element_type=jnp.float32,
                )
                for r in range(parts)
            )
            cosine, sine = cos_ref[s, :, lanes], sin_ref[s, :, lanes]
            real_part = real * cosine - imag * sine
            imag_part = real * sine + imag * cosine
            real_sum = real_part if s == 0 else real_sum + real_part
            imag_sum = imag_part if s == 0 else imag_sum + imag_part
        for k in range(width // LANES):
            piece = slice(k * LANES, (k + 1) * LANES)
            store(start // LANES + k, 0, real_sum[:, piece])
            store(start // LANES + k, 1, imag_sum[:, piece])


def root_kernel(
    pattern_hbm, phi_ref, theta_ref, offsets_ref, row_ref, column_ref, out_ref,
    pattern_ref, cos_ref, sin_ref, coarse_ref, sums,
    core_in, low_first, high_first, high_second, low_second, far_in,
    load_sem, core_sem, first_sem, second_sem, far_sem,
):
    chunks, _, n_high, _, n_far, parts, per_chunk, band_theta, _ = sums.shape
    group = pattern_ref.shape[3]
    phi, theta = lax.axis_index("phi"), lax.axis_index("theta")
    high, low = phi // 2, lax.rem(phi, 2)
    far, core = theta // 2, lax.rem(theta, 2)

    def turned(index, step, count):
        return lax.rem(index + step, count)

    core_peer = (phi, far * 2 + 1 - core)
    low_peer = (high * 2 + 1 - low, theta)

    def high_peer(step):
        return (turned(high, step, n_high) * 2 + low, theta)

    def far_peer(step):
        return (phi, turned(far, step, n_far) * 2 + core)

    def send(source, target, sems, peer):
        return pltpu.make_async_remote_copy(
            src_ref=source,
            dst_ref=target,
            send_sem=sems.at[0],
            recv_sem=sems.at[1],
            device_id=peer,
            device_id_type=pl.DeviceIdType.MESH,
        )

    def core_copies(k):
        return [send(sums.at[k, 1 - core], core_in.at[k], core_sem.at[k], core_peer)]

    def first_copies(k, parity):
        if parity == 0:
            source = sums.at[k, core, :, 1 - low]
            return [send(source, low_first.at[k // 2], first_sem.at[k, 0], low_peer)]
        return [
            send(
                sums.at[k, core, turned(high, d, n_high)],
                high_first.at[k // 2, d - 1],
                first_sem.at[k, d - 1],
                high_peer(d),
            )
            for d in range(1, n_high)
        ]

    def second_copies(k, parity):
        if parity == 1:
            source = sums.at[k, core, high, 1 - low]
            return [send(source, low_second.at[k // 2], second_sem.at[k, 0], low_peer)]
        return [
            send(
                sums.at[k, core, turned(high, d, n_high), low],
                high_second.at[k // 2, d - 1],
                second_sem.at[k, d - 1],
                high_peer(d),
            )
            for d in range(1, n_high)
        ]

    def far_copies(k):
        return [
            send(
                sums.at[k, core, high, low, turned(far, d, n_far)],
                far_in.at[k, d - 1],
                far_sem.at[k, d - 1],
                far_peer(d),
            )
            for d in range(1, n_far)
        ]

    def start(copies):
        for copy in copies:
            copy.start()

    def arrive(copies):
        for copy in copies:
            copy.wait_recv()

    def after_core(k, parity):
        arrive(core_copies(k))
        sums[k, core] = sums[k, core] + core_in[k]
        start(first_copies(k, parity))

    def after_first(k, parity):
        arrive(first_copies(k, parity))
        if parity == 0:
            for h in range(n_high):
                sums[k, core, h, low] = sums[k, core, h, low] + low_first[k // 2, h]
        else:
            total = sums[k, core, high]
            for d in range(1, n_high):
                total = total + high_first[k // 2, d - 1]
            sums[k, core, high] = total
        start(second_copies(k, parity))

    def after_second(k, parity):
        arrive(second_copies(k, parity))
        total = sums[k, core, high, low]
        if parity == 1:
            total = total + low_second[k // 2]
        else:
            for d in range(1, n_high):
                total = total + high_second[k // 2, d - 1]
        sums[k, core, high, low] = total
        start(far_copies(k))

    def load(k):
        return pltpu.make_async_copy(
            pattern_hbm.at[:, :, :, pl.ds(k * per_chunk, per_chunk)],
            pattern_ref.at[k],
            load_sem.at[k],
        )

    for k in range(chunks):
        load(k).start()

    peers = [core_peer, low_peer]
    peers += [high_peer(d) for d in range(1, n_high)] + [far_peer(d) for d in range(1, n_far)]
    barrier = pltpu.get_barrier_semaphore()
    for peer in peers:
        pl.semaphore_signal(barrier, inc=1, device_id=peer, device_id_type=pl.DeviceIdType.MESH)
    phase_factors(offsets_ref, row_ref, column_ref, cos_ref, sin_ref)
    pl.semaphore_wait(barrier, len(peers))

    def compute(k):
        load(k).wait()

        @pl.loop(0, per_chunk)
        def _(unit):
            def pattern(s, r):
                return jnp.concatenate(
                    [pattern_ref[k, s, r, g, unit] for g in range(group)], axis=1
                )

            def store(band, part, value):
                value = value.reshape(n_far, 2, band_theta, LANES)
                for c in range(2):
                    sums[k, c, band // 2, band % 2, :, part, unit] = value[:, c]

            subtree_sum(pattern, phi_ref, theta_ref, coarse_ref, cos_ref, sin_ref, store)

    stages = ((1, after_core), (FIRST_LAG, after_first), (SECOND_LAG, after_second))

    @pl.loop(0, chunks // 2)
    def _(pair):
        for parity in range(2):
            k = pair * 2 + parity
            compute(k)
            start(core_copies(k))
            for lag, stage in stages[::-1]:

                @pl.when(k >= lag)
                def _(lag=lag, stage=stage, k=k, parity=parity):
                    stage(k - lag, (parity - lag) % 2)

    for step in range(chunks, chunks + SECOND_LAG):
        for lag, stage in stages[::-1]:
            if step - lag < chunks:
                stage(step - lag, (step - lag) % 2)

    for k in range(chunks):
        arrive(far_copies(k))
        total = sums[k, core, high, low, far]
        for d in range(1, n_far):
            total = total + far_in[k, d - 1]
        out_ref[:, k * per_chunk : (k + 1) * per_chunk] = total

    @pl.loop(0, chunks // 2)
    def _(pair):
        for parity in range(2):
            k = pair * 2 + parity
            copies = core_copies(k) + first_copies(k, parity) + second_copies(k, parity)
            for copy in copies + far_copies(k):
                copy.wait_send()


def root_tile(pattern, up_phi_grouped, up_theta, offsets, count_phi, count_theta):
    held, parts, group, units, polar, azimuth = pattern.shape
    rows, columns = direction_tables(group, count_phi)
    band_theta = NT // count_theta
    n_high, n_far = count_phi // 2, count_theta // 2
    chunks = min(CHUNKS, units)
    per_chunk = units // chunks
    tile = (parts, per_chunk, band_theta, LANES)
    whole = pl.BlockSpec(memory_space=pltpu.VMEM)
    peers = max(1, n_high - 1)
    return pl.pallas_call(
        root_kernel,
        out_shape=jax.ShapeDtypeStruct((parts, units, band_theta, LANES), jnp.float32),
        in_specs=[
            pl.BlockSpec(memory_space=pl.ANY), whole, whole,
            pl.BlockSpec(memory_space=pltpu.SMEM), whole, whole,
        ],
        out_specs=whole,
        scratch_shapes=[
            pltpu.VMEM((chunks, held, parts, group, per_chunk, polar, azimuth), jnp.bfloat16),
            pltpu.VMEM((held, NT, count_phi * LANES), jnp.float32),
            pltpu.VMEM((held, NT, count_phi * LANES), jnp.float32),
            pltpu.VMEM((held * parts * polar, count_phi * LANES), jnp.bfloat16),
            pltpu.VMEM((chunks, 2, n_high, 2, n_far) + tile, jnp.float32),
            pltpu.VMEM((chunks, n_high, 2, n_far) + tile, jnp.float32),
            pltpu.VMEM((chunks // 2, n_high, n_far) + tile, jnp.float32),
            pltpu.VMEM((chunks // 2, peers, 2, n_far) + tile, jnp.float32),
            pltpu.VMEM((chunks // 2, peers, n_far) + tile, jnp.float32),
            pltpu.VMEM((chunks // 2, n_far) + tile, jnp.float32),
            pltpu.VMEM((chunks, n_far - 1) + tile, jnp.float32),
            pltpu.SemaphoreType.DMA((chunks,)),
            pltpu.SemaphoreType.DMA((chunks, 2)),
            pltpu.SemaphoreType.DMA((chunks, peers, 2)),
            pltpu.SemaphoreType.DMA((chunks, peers, 2)),
            pltpu.SemaphoreType.DMA((chunks, n_far - 1, 2)),
        ],
        compiler_params=pltpu.CompilerParams(
            vmem_limit_bytes=60 << 20, collective_id=0, has_side_effects=True
        ),
    )(pattern, up_phi_grouped, up_theta, offsets, jnp.asarray(rows), jnp.asarray(columns))


def lagrange_matrix(start, frac, width):
    position = 1.0 + frac
    weights = [
        -(position - 1.0) * (position - 2.0) * (position - 3.0) / 6.0,
        position * (position - 2.0) * (position - 3.0) / 2.0,
        -position * (position - 1.0) * (position - 3.0) / 2.0,
        position * (position - 1.0) * (position - 2.0) / 6.0,
    ]
    columns = jnp.arange(width, dtype=jnp.int32)[None, :]
    matrix = jnp.zeros((start.shape[0], width), jnp.float32)
    for tap in range(4):
        matrix = matrix + jnp.where(columns == (start + tap)[:, None], weights[tap][:, None], 0.0)
    return matrix


def per_device(
    subtree_pattern, up_phi, up_theta, offsets, theta_start, theta_frac, phi_start, phi_frac
):
    count_phi = lax.axis_size("phi")
    count_theta = lax.axis_size("theta")
    band_theta = NT // count_theta
    band_phi = NP // count_phi
    group = LANES // band_phi
    held, parts, channels, polar, azimuth = subtree_pattern.shape
    units = channels // group
    pattern = subtree_pattern.reshape(held, parts, group, units, polar, azimuth)
    up_phi_grouped = grouped_up_phi(up_phi, group, count_phi)
    root = root_tile(pattern, up_phi_grouped, up_theta, offsets, count_phi, count_theta)
    root = root.reshape(parts, units, band_theta, group, band_phi)
    root = root.transpose(0, 3, 1, 2, 4).reshape(parts, channels, band_theta, band_phi)
    padded = padded_2(root, (("theta", 2),), 2, False)
    padded = padded_2(padded, (("phi", 3),), 2, True)
    local_theta = theta_start - lax.axis_index("theta") * band_theta + 2
    local_phi = phi_start - lax.axis_index("phi") * band_phi + 2
    theta_weights = lagrange_matrix(local_theta, theta_frac, band_theta + 4)
    phi_weights = lagrange_matrix(local_phi, phi_frac, band_phi + 4)
    field = jnp.einsum("ot,rqtp->rqop", theta_weights, padded, precision=lax.Precision.HIGHEST)
    field = jnp.einsum("rqop,wp->rqow", field, phi_weights, precision=lax.Precision.HIGHEST)
    subtrees = held * count_phi * count_theta
    power = (field * field).reshape(4, channels // 2, field.shape[2], field.shape[3])
    return jnp.sum(power, axis=0) / subtrees


def solution(mesh):
    return jax.shard_map(
        per_device,
        mesh=mesh,
        in_specs=(
            P(("phi", "theta"), None, None, None, None),
            P(),
            P(),
            P(None, ("phi", "theta")),
            P("theta"),
            P("theta"),
            P("phi"),
            P("phi"),
        ),
        out_specs=P(None, "theta", "phi"),
        check_vma=False,
    )
```

```python
import math

import jax
import jax.numpy as jnp
import numpy as np
from jax import lax
from jax.experimental import pallas as pl
from jax.experimental.pallas import tpu as pltpu
from jax.sharding import PartitionSpec as P

NT = 128
NP = 256
LANES = 128
CHUNKS = 8
FIRST_LAG = 3
SECOND_LAG = 5


def direction_tables(group, bands):
    polar = (np.arange(NT) + 0.5) * (math.pi / NT)
    rows = np.stack([np.sin(polar), np.cos(polar)])[:, :, None]
    rows = np.broadcast_to(rows, (2, NT, LANES))
    azimuth = (np.arange(NP) * (2.0 * math.pi / NP)).reshape(bands, 1, -1)
    azimuth = np.broadcast_to(azimuth, (bands, group, azimuth.shape[2])).reshape(1, -1)
    columns = np.stack([np.cos(azimuth), np.sin(azimuth)])
    columns = np.broadcast_to(columns, (2, 8, columns.shape[2]))
    return rows.astype(np.float32), columns.astype(np.float32)


def grouped_up_phi(up_phi, group, bands):
    split = up_phi.reshape(up_phi.shape[0], bands, 1, NP // bands)
    blocks = []
    for g in range(group):
        pads = [(0, 0), (0, 0), (g, group - 1 - g), (0, 0)]
        blocks.append(jnp.pad(split, pads).reshape(up_phi.shape[0], -1))
    return jnp.concatenate(blocks, axis=0)


def turn_series():
    two_pi = 2.0 * math.pi
    sine = [(-1) ** k * two_pi ** (2 * k + 1) / math.factorial(2 * k + 1) for k in range(9)]
    cosine = [(-1) ** k * two_pi ** (2 * k) / math.factorial(2 * k) for k in range(10)]
    return sine, cosine


def horner(square, terms):
    value = jnp.full_like(square, terms[-1])
    for term in terms[-2::-1]:
        value = value * square + term
    return value


def phase_factors(offsets_ref, row_ref, column_ref, cos_ref, sin_ref):
    sine_terms, cosine_terms = turn_series()
    lane_groups = cos_ref.shape[2] // LANES

    @pl.loop(0, cos_ref.shape[0])
    def _(s):
        off_x, off_y, off_z = (offsets_ref[k, s] for k in range(3))
        for lane in range(lane_groups):
            lanes = slice(lane * LANES, (lane + 1) * LANES)
            wave = off_x * column_ref[0, 0:1, lanes] + off_y * column_ref[1, 0:1, lanes]
            turns = wave * row_ref[0] + off_z * row_ref[1]
            turns = turns - jnp.floor(turns + 0.5)
            square = turns * turns
            cos_ref[s, :, lanes] = horner(square, cosine_terms)
            sin_ref[s, :, lanes] = horner(square, sine_terms) * turns


def subtree_sum(pattern, phi_ref, theta_ref, coarse_ref, cos_ref, sin_ref, store):
    count, polar = cos_ref.shape[0], theta_ref.shape[1]
    parts = coarse_ref.shape[0] // (count * polar)
    rows = [pattern(s, r) for s in range(count) for r in range(parts)]
    coarse_ref[...] = jnp.dot(
        jnp.concatenate(rows, axis=0), phi_ref[...], preferred_element_type=jnp.float32
    ).astype(jnp.bfloat16)
    width = 2 * LANES
    for start in range(0, phi_ref.shape[1], width):
        lanes = slice(start, start + width)
        real_sum, imag_sum = None, None
        for s in range(count):
            real, imag = (
                jnp.dot(
                    theta_ref[...],
                    coarse_ref[(s * parts + r) * polar : (s * parts + r + 1) * polar, lanes],
                    preferred_element_type=jnp.float32,
                )
                for r in range(parts)
            )
            cosine, sine = cos_ref[s, :, lanes], sin_ref[s, :, lanes]
            real_part = real * cosine - imag * sine
            imag_part = real * sine + imag * cosine
            real_sum = real_part if s == 0 else real_sum + real_part
            imag_sum = imag_part if s == 0 else imag_sum + imag_part
        for k in range(width // LANES):
            piece = slice(k * LANES, (k + 1) * LANES)
            store(start // LANES + k, 0, real_sum[:, piece])
            store(start // LANES + k, 1, imag_sum[:, piece])


def tap_weights(start, frac, node):
    position = 1.0 + frac
    weights = [
        -(position - 1.0) * (position - 2.0) * (position - 3.0) / 6.0,
        position * (position - 2.0) * (position - 3.0) / 2.0,
        -position * (position - 1.0) * (position - 3.0) / 2.0,
        position * (position - 1.0) * (position - 2.0) / 6.0,
    ]
    matrix = jnp.zeros(node.shape, jnp.float32)
    for tap in range(4):
        matrix = matrix + jnp.where(node == start + tap, weights[tap], 0.0)
    return matrix


def split_dot(a, b):
    a_high, b_high = a.astype(jnp.bfloat16), b.astype(jnp.bfloat16)
    a_low = (a - a_high.astype(jnp.float32)).astype(jnp.bfloat16)
    b_low = (b - b_high.astype(jnp.float32)).astype(jnp.bfloat16)

    def dot(left, right):
        return jnp.dot(left, right, preferred_element_type=jnp.float32)

    return dot(a_high, b_high) + (dot(a_high, b_low) + dot(a_low, b_high))


def root_kernel(
    pattern_hbm, phi_ref, theta_ref, offsets_ref, row_ref, column_ref,
    theta_start_ref, theta_frac_ref, phi_start_ref, phi_frac_ref, out_ref,
    pattern_ref, cos_ref, sin_ref, coarse_ref, sums,
    core_in, low_first, high_first, high_second, low_second, far_in,
    root, row_low, row_high, edges, edge_left, edge_right, weights_ref,
    load_sem, core_sem, first_sem, second_sem, far_sem, row_sem, edge_sem,
):
    chunks, _, n_high, _, n_far, parts, per_chunk, band_theta, _ = sums.shape
    group = pattern_ref.shape[3]
    phi, theta = lax.axis_index("phi"), lax.axis_index("theta")
    high, low = phi // 2, lax.rem(phi, 2)
    far, core = theta // 2, lax.rem(theta, 2)

    def turned(index, step, count):
        return lax.rem(index + step, count)

    core_peer = (phi, far * 2 + 1 - core)
    low_peer = (high * 2 + 1 - low, theta)

    def high_peer(step):
        return (turned(high, step, n_high) * 2 + low, theta)

    def far_peer(step):
        return (phi, turned(far, step, n_far) * 2 + core)

    def send(source, target, sems, peer):
        return pltpu.make_async_remote_copy(
            src_ref=source,
            dst_ref=target,
            send_sem=sems.at[0],
            recv_sem=sems.at[1],
            device_id=peer,
            device_id_type=pl.DeviceIdType.MESH,
        )

    def core_copies(k):
        return [send(sums.at[k, 1 - core], core_in.at[k], core_sem.at[k], core_peer)]

    def first_copies(k, parity):
        if parity == 0:
            source = sums.at[k, core, :, 1 - low]
            return [send(source, low_first.at[k // 2], first_sem.at[k, 0], low_peer)]
        return [
            send(
                sums.at[k, core, turned(high, d, n_high)],
                high_first.at[k // 2, d - 1],
                first_sem.at[k, d - 1],
                high_peer(d),
            )
            for d in range(1, n_high)
        ]

    def second_copies(k, parity):
        if parity == 1:
            source = sums.at[k, core, high, 1 - low]
            return [send(source, low_second.at[k // 2], second_sem.at[k, 0], low_peer)]
        return [
            send(
                sums.at[k, core, turned(high, d, n_high), low],
                high_second.at[k // 2, d - 1],
                second_sem.at[k, d - 1],
                high_peer(d),
            )
            for d in range(1, n_high)
        ]

    def far_copies(k):
        return [
            send(
                sums.at[k, core, high, low, turned(far, d, n_far)],
                far_in.at[k, d - 1],
                far_sem.at[k, d - 1],
                far_peer(d),
            )
            for d in range(1, n_far)
        ]

    count_phi, count_theta = n_high * 2, n_far * 2
    before = (phi, lax.rem(theta + count_theta - 1, count_theta))
    after = (phi, lax.rem(theta + 1, count_theta))
    left = (lax.rem(phi + count_phi - 1, count_phi), theta)
    right = (lax.rem(phi + 1, count_phi), theta)

    def row_to_after(k):
        return send(
            root.at[k, :, :, pl.ds(band_theta - 8, 8)], row_low.at[k], row_sem.at[k, 0], after
        )

    def row_to_before(k):
        return send(root.at[k, :, :, pl.ds(0, 8)], row_high.at[k], row_sem.at[k, 1], before)

    def start(copies):
        for copy in copies:
            copy.start()

    def arrive(copies):
        for copy in copies:
            copy.wait_recv()

    def after_core(k, parity):
        arrive(core_copies(k))
        sums[k, core] = sums[k, core] + core_in[k]
        start(first_copies(k, parity))

    def after_first(k, parity):
        arrive(first_copies(k, parity))
        if parity == 0:
            for h in range(n_high):
                sums[k, core, h, low] = sums[k, core, h, low] + low_first[k // 2, h]
        else:
            total = sums[k, core, high]
            for d in range(1, n_high):
                total = total + high_first[k // 2, d - 1]
            sums[k, core, high] = total
        start(second_copies(k, parity))

    def after_second(k, parity):
        arrive(second_copies(k, parity))
        total = sums[k, core, high, low]
        if parity == 1:
            total = total + low_second[k // 2]
        else:
            for d in range(1, n_high):
                total = total + high_second[k // 2, d - 1]
        sums[k, core, high, low] = total
        start(far_copies(k))

    def load(k):
        return pltpu.make_async_copy(
            pattern_hbm.at[:, :, :, pl.ds(k * per_chunk, per_chunk)],
            pattern_ref.at[k],
            load_sem.at[k],
        )

    for k in range(chunks):
        load(k).start()

    peers = [core_peer, low_peer]
    peers += [high_peer(d) for d in range(1, n_high)] + [far_peer(d) for d in range(1, n_far)]
    peers += [before, after, left, right]
    barrier = pltpu.get_barrier_semaphore()
    for peer in peers:
        pl.semaphore_signal(barrier, inc=1, device_id=peer, device_id_type=pl.DeviceIdType.MESH)
    phase_factors(offsets_ref, row_ref, column_ref, cos_ref, sin_ref)
    pl.semaphore_wait(barrier, len(peers))

    def compute(k):
        load(k).wait()

        @pl.loop(0, per_chunk)
        def _(unit):
            def pattern(s, r):
                return jnp.concatenate(
                    [pattern_ref[k, s, r, g, unit] for g in range(group)], axis=1
                )

            def store(band, part, value):
                value = value.reshape(n_far, 2, band_theta, LANES)
                for c in range(2):
                    sums[k, c, band // 2, band % 2, :, part, unit] = value[:, c]

            subtree_sum(pattern, phi_ref, theta_ref, coarse_ref, cos_ref, sin_ref, store)

    stages = ((1, after_core), (FIRST_LAG, after_first), (SECOND_LAG, after_second))

    @pl.loop(0, chunks // 2)
    def _(pair):
        for parity in range(2):
            k = pair * 2 + parity
            compute(k)
            start(core_copies(k))
            for lag, stage in stages[::-1]:

                @pl.when(k >= lag)
                def _(lag=lag, stage=stage, k=k, parity=parity):
                    stage(k - lag, (parity - lag) % 2)

    for step in range(chunks, chunks + SECOND_LAG):
        for lag, stage in stages[::-1]:
            if step - lag < chunks:
                stage(step - lag, (step - lag) % 2)

    for k in range(chunks):
        arrive(far_copies(k))
        total = sums[k, core, high, low, far]
        for d in range(1, n_far):
            total = total + far_in[k, d - 1]
        root[k] = total

        @pl.when(theta < count_theta - 1)
        def _(k=k):
            row_to_after(k).start()

        @pl.when(theta > 0)
        def _(k=k):
            row_to_before(k).start()

    @pl.when(theta > 0)
    def _():
        for k in range(chunks):
            row_to_after(k).wait_recv()

    @pl.when(theta == 0)
    def _():
        row_low[...] = jnp.zeros_like(row_low)

    @pl.when(theta < count_theta - 1)
    def _():
        for k in range(chunks):
            row_to_before(k).wait_recv()

    @pl.when(theta == count_theta - 1)
    def _():
        row_high[...] = jnp.zeros_like(row_high)

    units = chunks * per_chunk
    planes = [(r, k, u) for r in range(parts) for k in range(chunks) for u in range(per_chunk)]
    stacked = jnp.concatenate(
        [
            jnp.concatenate([row_low[k, r, u], root[k, r, u], row_high[k, r, u]], axis=0)
            for r, k, u in planes
        ],
        axis=1,
    )
    polar_weights = tap_weights(
        theta_start_ref[...] - theta * band_theta + 8,
        theta_frac_ref[...],
        lax.broadcasted_iota(jnp.int32, (theta_start_ref.shape[0], band_theta + 16), 1),
    )
    rows = split_dot(polar_weights, stacked)

    band_phi = LANES // group
    lane = lax.broadcasted_iota(jnp.int32, (rows.shape[0], LANES), 1)
    own = 4 * group
    per_pack = LANES // own
    plane = [rows[:, j * LANES : (j + 1) * LANES] for j in range(len(planes))]
    for pack in range(len(planes) // per_pack):
        packed = jnp.zeros_like(plane[0])
        for j in range(per_pack):
            for g in range(group):
                at = own * j + 4 * g
                shift = (at - (g * band_phi - 2)) % LANES
                value = plane[pack * per_pack + j]
                value = pltpu.roll(value, shift, 1) if shift else value
                packed = jnp.where((lane >= at) & (lane < at + 4), value, packed)
        edges[pack] = packed
    to_right = send(edges, edge_left, edge_sem.at[0], right)
    to_left = send(edges, edge_right, edge_sem.at[1], left)
    to_right.start()
    to_left.start()

    width = phi_start_ref.shape[1]
    local_start = phi_start_ref[...] - phi * band_phi
    row = lax.broadcasted_iota(jnp.int32, (LANES, width), 0)
    own_group, own_node = row // band_phi, lax.rem(row, band_phi)
    slot = lax.rem(row, own) // 4
    offset = lax.rem(row, 4)
    from_left = (row < own) & (offset < 2)
    from_right = (row >= own) & (row < 2 * own) & (offset >= 2)
    edge_group = jnp.where(from_left, lax.rem(slot + group - 1, group), slot)
    edge_node = jnp.where(from_left, offset - 2, band_phi + offset - 2)
    own_taps = tap_weights(local_start, phi_frac_ref[...], own_node)
    edge_taps = tap_weights(local_start, phi_frac_ref[...], edge_node)
    edge_taps = jnp.where(from_left | from_right, edge_taps, 0.0)
    for g in range(group):
        columns = slice(g * width, (g + 1) * width)
        weights_ref[:LANES, columns] = jnp.where(own_group == g, own_taps, 0.0)
        weights_ref[LANES:, columns] = jnp.where(edge_group == g, edge_taps, 0.0)

    to_right.wait_recv()
    to_left.wait_recv()
    operand = []
    for j in range(len(planes)):
        pack, place = j // per_pack, j % per_pack
        from_l, from_r = edge_left[pack], edge_right[pack]
        shift_l, shift_r = (-own * place) % LANES, (own - own * place) % LANES
        from_l = pltpu.roll(from_l, shift_l, 1) if shift_l else from_l
        from_r = pltpu.roll(from_r, shift_r, 1) if shift_r else from_r
        operand.append(jnp.concatenate([plane[j], jnp.where(lane < own, from_l, from_r)], axis=1))
    field = split_dot(jnp.concatenate(operand, axis=0), weights_ref[...])
    incidences = out_ref.shape[0]
    height = rows.shape[0]
    power = [None] * incidences
    for j in range(len(planes)):
        for g in range(group):
            value = field[j * height : (j + 1) * height, g * width : (g + 1) * width]
            at = (g * units + j % units) % incidences
            power[at] = value * value if power[at] is None else power[at] + value * value
    for at in range(incidences):
        out_ref[at] = power[at]

    to_right.wait_send()
    to_left.wait_send()

    @pl.when(theta < count_theta - 1)
    def _():
        for k in range(chunks):
            row_to_after(k).wait_send()

    @pl.when(theta > 0)
    def _():
        for k in range(chunks):
            row_to_before(k).wait_send()

    @pl.loop(0, chunks // 2)
    def _(pair):
        for parity in range(2):
            k = pair * 2 + parity
            copies = core_copies(k) + first_copies(k, parity) + second_copies(k, parity)
            for copy in copies + far_copies(k):
                copy.wait_send()


def power_sum(
    pattern, up_phi_grouped, up_theta, offsets, rows_out, columns_out, count_phi, count_theta
):
    held, parts, group, units, polar, azimuth = pattern.shape
    rows, columns = direction_tables(group, count_phi)
    band_theta = NT // count_theta
    n_high, n_far = count_phi // 2, count_theta // 2
    chunks = min(CHUNKS, units)
    per_chunk = units // chunks
    tile = (parts, per_chunk, band_theta, LANES)
    whole = pl.BlockSpec(memory_space=pltpu.VMEM)
    peers = max(1, n_high - 1)
    height, width = rows_out[0].shape[0], columns_out[0].shape[0]
    channels = group * units
    packs = parts * channels * 4 // LANES
    return pl.pallas_call(
        root_kernel,
        out_shape=jax.ShapeDtypeStruct((channels // 2, height, width), jnp.float32),
        in_specs=[
            pl.BlockSpec(memory_space=pl.ANY), whole, whole,
            pl.BlockSpec(memory_space=pltpu.SMEM), whole, whole, whole, whole, whole, whole,
        ],
        out_specs=whole,
        scratch_shapes=[
            pltpu.VMEM((chunks, held, parts, group, per_chunk, polar, azimuth), jnp.bfloat16),
            pltpu.VMEM((held, NT, count_phi * LANES), jnp.float32),
            pltpu.VMEM((held, NT, count_phi * LANES), jnp.float32),
            pltpu.VMEM((held * parts * polar, count_phi * LANES), jnp.bfloat16),
            pltpu.VMEM((chunks, 2, n_high, 2, n_far) + tile, jnp.float32),
            pltpu.VMEM((chunks, n_high, 2, n_far) + tile, jnp.float32),
            pltpu.VMEM((chunks // 2, n_high, n_far) + tile, jnp.float32),
            pltpu.VMEM((chunks // 2, peers, 2, n_far) + tile, jnp.float32),
            pltpu.VMEM((chunks // 2, peers, n_far) + tile, jnp.float32),
            pltpu.VMEM((chunks // 2, n_far) + tile, jnp.float32),
            pltpu.VMEM((chunks, n_far - 1) + tile, jnp.float32),
            pltpu.VMEM((chunks,) + tile, jnp.float32),
            pltpu.VMEM((chunks, parts, per_chunk, 8, LANES), jnp.float32),
            pltpu.VMEM((chunks, parts, per_chunk, 8, LANES), jnp.float32),
            pltpu.VMEM((packs, height, LANES), jnp.float32),
            pltpu.VMEM((packs, height, LANES), jnp.float32),
            pltpu.VMEM((packs, height, LANES), jnp.float32),
            pltpu.VMEM((2 * LANES, group * width), jnp.float32),
            pltpu.SemaphoreType.DMA((chunks,)),
            pltpu.SemaphoreType.DMA((chunks, 2)),
            pltpu.SemaphoreType.DMA((chunks, peers, 2)),
            pltpu.SemaphoreType.DMA((chunks, peers, 2)),
            pltpu.SemaphoreType.DMA((chunks, n_far - 1, 2)),
            pltpu.SemaphoreType.DMA((chunks, 2, 2)),
            pltpu.SemaphoreType.DMA((2, 2)),
        ],
        compiler_params=pltpu.CompilerParams(
            vmem_limit_bytes=60 << 20, collective_id=0, has_side_effects=True
        ),
    )(
        pattern, up_phi_grouped, up_theta, offsets, jnp.asarray(rows), jnp.asarray(columns),
        *(value[:, None] for value in rows_out), *(value[None, :] for value in columns_out),
    )


def per_device(
    subtree_pattern, up_phi, up_theta, offsets, theta_start, theta_frac, phi_start, phi_frac
):
    count_phi = lax.axis_size("phi")
    count_theta = lax.axis_size("theta")
    group = LANES * count_phi // NP
    held, parts, channels, polar, azimuth = subtree_pattern.shape
    units = channels // group
    pattern = subtree_pattern.reshape(held, parts, group, units, polar, azimuth)
    up_phi_grouped = grouped_up_phi(up_phi, group, count_phi)
    power = power_sum(
        pattern, up_phi_grouped, up_theta, offsets,
        (theta_start, theta_frac), (phi_start, phi_frac), count_phi, count_theta,
    )
    return power / (held * count_phi * count_theta)


def solution(mesh):
    return jax.shard_map(
        per_device,
        mesh=mesh,
        in_specs=(
            P(("phi", "theta"), None, None, None, None),
            P(),
            P(),
            P(None, ("phi", "theta")),
            P("theta"),
            P("theta"),
            P("phi"),
            P("phi"),
        ),
        out_specs=P(None, "theta", "phi"),
        check_vma=False,
    )
```

```python
import math

import jax
import jax.numpy as jnp
import numpy as np
from jax import lax
from jax.experimental import pallas as pl
from jax.experimental.pallas import tpu as pltpu
from jax.sharding import PartitionSpec as P

NT = 128
NP = 256
LANES = 128
CHUNKS = 16
FIRST_LAG = 4
SECOND_LAG = 8


def direction_tables(group, bands):
    polar = (np.arange(NT) + 0.5) * (math.pi / NT)
    rows = np.stack([np.sin(polar), np.cos(polar)])[:, :, None]
    rows = np.broadcast_to(rows, (2, NT, LANES))
    azimuth = (np.arange(NP) * (2.0 * math.pi / NP)).reshape(bands, 1, -1)
    azimuth = np.broadcast_to(azimuth, (bands, group, azimuth.shape[2])).reshape(1, -1)
    columns = np.stack([np.cos(azimuth), np.sin(azimuth)])
    columns = np.broadcast_to(columns, (2, 8, columns.shape[2]))
    return rows.astype(np.float32), columns.astype(np.float32)


def group_up_phi(source_ref, target_ref, group, bands):
    depth, band = source_ref.shape[0], NP // bands
    lane = lax.broadcasted_iota(jnp.int32, (depth, LANES), 1)
    for a in range(bands):
        tile, inside = divmod(a * band, LANES)
        columns = source_ref[:, tile * LANES : (tile + 1) * LANES].astype(jnp.float32)
        for g in range(group):
            shift = (g * band - inside) % LANES
            value = pltpu.roll(columns, shift, 1) if shift else columns
            value = jnp.where((lane >= g * band) & (lane < (g + 1) * band), value, 0.0)
            target_ref[g * depth : (g + 1) * depth, a * LANES : (a + 1) * LANES] = value.astype(
                jnp.bfloat16
            )


def turn_series():
    two_pi = 2.0 * math.pi
    sine = [(-1) ** k * two_pi ** (2 * k + 1) / math.factorial(2 * k + 1) for k in range(9)]
    cosine = [(-1) ** k * two_pi ** (2 * k) / math.factorial(2 * k) for k in range(10)]
    return sine, cosine


def horner(square, terms):
    value = jnp.full_like(square, terms[-1])
    for term in terms[-2::-1]:
        value = value * square + term
    return value


def phase_factors(offsets_ref, row_ref, column_ref, cos_ref, sin_ref):
    sine_terms, cosine_terms = turn_series()
    lane_groups = cos_ref.shape[2] // LANES

    @pl.loop(0, cos_ref.shape[0])
    def _(s):
        off_x, off_y, off_z = (offsets_ref[k, s] for k in range(3))
        for lane in range(lane_groups):
            lanes = slice(lane * LANES, (lane + 1) * LANES)
            wave = off_x * column_ref[0, 0:1, lanes] + off_y * column_ref[1, 0:1, lanes]
            turns = wave * row_ref[0] + off_z * row_ref[1]
            turns = turns - jnp.floor(turns + 0.5)
            square = turns * turns
            cos_ref[s, :, lanes] = horner(square, cosine_terms)
            sin_ref[s, :, lanes] = horner(square, sine_terms) * turns


def subtree_sum(pattern, phi_ref, theta_ref, coarse_ref, cos_ref, sin_ref, store):
    count, polar = cos_ref.shape[0], theta_ref.shape[1]
    parts = coarse_ref.shape[0] // (count * polar)
    rows = [pattern(s, r) for s in range(count) for r in range(parts)]
    coarse_ref[...] = jnp.dot(
        jnp.concatenate(rows, axis=0), phi_ref[...], preferred_element_type=jnp.float32
    ).astype(jnp.bfloat16)
    width = 2 * LANES
    for start in range(0, phi_ref.shape[1], width):
        lanes = slice(start, start + width)
        real_sum, imag_sum = None, None
        for s in range(count):
            real, imag = (
                jnp.dot(
                    theta_ref[...],
                    coarse_ref[(s * parts + r) * polar : (s * parts + r + 1) * polar, lanes],
                    preferred_element_type=jnp.float32,
                )
                for r in range(parts)
            )
            cosine, sine = cos_ref[s, :, lanes], sin_ref[s, :, lanes]
            real_part = real * cosine - imag * sine
            imag_part = real * sine + imag * cosine
            real_sum = real_part if s == 0 else real_sum + real_part
            imag_sum = imag_part if s == 0 else imag_sum + imag_part
        for k in range(width // LANES):
            piece = slice(k * LANES, (k + 1) * LANES)
            store(start // LANES + k, 0, real_sum[:, piece])
            store(start // LANES + k, 1, imag_sum[:, piece])


def tap_weights(start, frac, node):
    position = 1.0 + frac
    weights = [
        -(position - 1.0) * (position - 2.0) * (position - 3.0) / 6.0,
        position * (position - 2.0) * (position - 3.0) / 2.0,
        -position * (position - 1.0) * (position - 3.0) / 2.0,
        position * (position - 1.0) * (position - 2.0) / 6.0,
    ]
    matrix = jnp.zeros(node.shape, jnp.float32)
    for tap in range(4):
        matrix = matrix + jnp.where(node == start + tap, weights[tap], 0.0)
    return matrix


def split_dot(a, b, a_depth=1):
    a_high, b_high = a.astype(jnp.bfloat16), b.astype(jnp.bfloat16)
    a_low = (a - a_high.astype(jnp.float32)).astype(jnp.bfloat16)
    b_low = (b - b_high.astype(jnp.float32)).astype(jnp.bfloat16)

    def dot(left, right):
        numbers = (((a_depth,), (0,)), ((), ()))
        return lax.dot_general(left, right, numbers, preferred_element_type=jnp.float32)

    return dot(a_high, b_high) + (dot(a_high, b_low) + dot(a_low, b_high))


def root_kernel(
    pattern_hbm, up_phi_ref, up_theta_ref, offsets_ref, row_ref, column_ref,
    theta_start_ref, theta_frac_ref, phi_start_ref, phi_frac_ref, out_ref,
    pattern_ref, phi_ref, theta_ref, cos_ref, sin_ref, coarse_ref, sums,
    core_in, low_first, high_first, high_second, low_second, far_in,
    root, row_low, row_high, edges, edge_left, edge_right, weights_ref,
    load_sem, core_sem, first_sem, second_sem, far_sem, row_sem, edge_sem,
):
    chunks, _, n_high, _, n_far, parts, per_chunk, band_theta, _ = sums.shape
    group = pattern_ref.shape[3]
    phi, theta = lax.axis_index("phi"), lax.axis_index("theta")
    high, low = phi // 2, lax.rem(phi, 2)
    far, core = theta // 2, lax.rem(theta, 2)

    def turned(index, step, count):
        return lax.rem(index + step, count)

    core_peer = (phi, far * 2 + 1 - core)
    low_peer = (high * 2 + 1 - low, theta)

    def high_peer(step):
        return (turned(high, step, n_high) * 2 + low, theta)

    def far_peer(step):
        return (phi, turned(far, step, n_far) * 2 + core)

    def send(source, target, sems, peer):
        return pltpu.make_async_remote_copy(
            src_ref=source,
            dst_ref=target,
            send_sem=sems.at[0],
            recv_sem=sems.at[1],
            device_id=peer,
            device_id_type=pl.DeviceIdType.MESH,
        )

    def core_copies(k):
        return [send(sums.at[k, 1 - core], core_in.at[k], core_sem.at[k], core_peer)]

    def first_copies(k, parity):
        if parity == 0:
            source = sums.at[k, core, :, 1 - low]
            return [send(source, low_first.at[k // 2], first_sem.at[k, 0], low_peer)]
        return [
            send(
                sums.at[k, core, turned(high, d, n_high)],
                high_first.at[k // 2, d - 1],
                first_sem.at[k, d - 1],
                high_peer(d),
            )
            for d in range(1, n_high)
        ]

    def second_copies(k, parity):
        if parity == 1:
            source = sums.at[k, core, high, 1 - low]
            return [send(source, low_second.at[k // 2], second_sem.at[k, 0], low_peer)]
        return [
            send(
                sums.at[k, core, turned(high, d, n_high), low],
                high_second.at[k // 2, d - 1],
                second_sem.at[k, d - 1],
                high_peer(d),
            )
            for d in range(1, n_high)
        ]

    def far_copies(k):
        return [
            send(
                sums.at[k, core, high, low, turned(far, d, n_far)],
                far_in.at[k, d - 1],
                far_sem.at[k, d - 1],
                far_peer(d),
            )
            for d in range(1, n_far)
        ]

    count_phi, count_theta = n_high * 2, n_far * 2
    before = (phi, lax.rem(theta + count_theta - 1, count_theta))
    after = (phi, lax.rem(theta + 1, count_theta))
    left = (lax.rem(phi + count_phi - 1, count_phi), theta)
    right = (lax.rem(phi + 1, count_phi), theta)

    def row_to_after(k):
        return send(
            root.at[k, :, :, pl.ds(band_theta - 8, 8)], row_low.at[k], row_sem.at[k, 0], after
        )

    def row_to_before(k):
        return send(root.at[k, :, :, pl.ds(0, 8)], row_high.at[k], row_sem.at[k, 1], before)

    def start(copies):
        for copy in copies:
            copy.start()

    def arrive(copies):
        for copy in copies:
            copy.wait_recv()

    def after_core(k, parity):
        arrive(core_copies(k))
        sums[k, core] = sums[k, core] + core_in[k]
        start(first_copies(k, parity))

    def after_first(k, parity):
        arrive(first_copies(k, parity))
        if parity == 0:
            for h in range(n_high):
                sums[k, core, h, low] = sums[k, core, h, low] + low_first[k // 2, h]
        else:
            total = sums[k, core, high]
            for d in range(1, n_high):
                total = total + high_first[k // 2, d - 1]
            sums[k, core, high] = total
        start(second_copies(k, parity))

    def after_second(k, parity):
        arrive(second_copies(k, parity))
        total = sums[k, core, high, low]
        if parity == 1:
            total = total + low_second[k // 2]
        else:
            for d in range(1, n_high):
                total = total + high_second[k // 2, d - 1]
        sums[k, core, high, low] = total
        start(far_copies(k))

    def load(k):
        return pltpu.make_async_copy(
            pattern_hbm.at[:, :, :, pl.ds(k * per_chunk, per_chunk)],
            pattern_ref.at[k],
            load_sem.at[k],
        )

    for k in range(chunks):
        load(k).start()

    peers = [core_peer, low_peer]
    peers += [high_peer(d) for d in range(1, n_high)] + [far_peer(d) for d in range(1, n_far)]
    peers += [before, after, left, right]
    barrier = pltpu.get_barrier_semaphore()
    for peer in peers:
        pl.semaphore_signal(barrier, inc=1, device_id=peer, device_id_type=pl.DeviceIdType.MESH)
    group_up_phi(up_phi_ref, phi_ref, group, n_high * 2)
    theta_ref[...] = up_theta_ref[...].astype(jnp.float32).T.astype(jnp.bfloat16)
    phase_factors(offsets_ref, row_ref, column_ref, cos_ref, sin_ref)
    pl.semaphore_wait(barrier, len(peers))

    def compute(k):
        load(k).wait()

        @pl.loop(0, per_chunk)
        def _(unit):
            def pattern(s, r):
                return jnp.concatenate(
                    [pattern_ref[k, s, r, g, unit] for g in range(group)], axis=1
                )

            def store(band, part, value):
                value = value.reshape(n_far, 2, band_theta, LANES)
                for c in range(2):
                    sums[k, c, band // 2, band % 2, :, part, unit] = value[:, c]

            subtree_sum(pattern, phi_ref, theta_ref, coarse_ref, cos_ref, sin_ref, store)

    stages = ((1, after_core), (FIRST_LAG, after_first), (SECOND_LAG, after_second))

    @pl.loop(0, chunks // 2)
    def _(pair):
        for parity in range(2):
            k = pair * 2 + parity
            compute(k)
            start(core_copies(k))
            for lag, stage in stages:

                @pl.when(k >= lag)
                def _(lag=lag, stage=stage, k=k, parity=parity):
                    stage(k - lag, (parity - lag) % 2)

    for step in range(chunks, chunks + SECOND_LAG):
        for lag, stage in stages:
            if step - lag < chunks:
                stage(step - lag, (step - lag) % 2)

    for k in range(chunks):
        arrive(far_copies(k))
        total = sums[k, core, high, low, far]
        for d in range(1, n_far):
            total = total + far_in[k, d - 1]
        root[k] = total

        @pl.when(theta < count_theta - 1)
        def _(k=k):
            row_to_after(k).start()

        @pl.when(theta > 0)
        def _(k=k):
            row_to_before(k).start()

    @pl.when(theta > 0)
    def _():
        for k in range(chunks):
            row_to_after(k).wait_recv()

    @pl.when(theta == 0)
    def _():
        row_low[...] = jnp.zeros_like(row_low)

    @pl.when(theta < count_theta - 1)
    def _():
        for k in range(chunks):
            row_to_before(k).wait_recv()

    @pl.when(theta == count_theta - 1)
    def _():
        row_high[...] = jnp.zeros_like(row_high)

    units = chunks * per_chunk
    planes = [(r, k, u) for r in range(parts) for k in range(chunks) for u in range(per_chunk)]
    stacked = jnp.concatenate(
        [
            jnp.concatenate([row_low[k, r, u], root[k, r, u], row_high[k, r, u]], axis=0)
            for r, k, u in planes
        ],
        axis=1,
    )
    polar_weights = tap_weights(
        theta_start_ref[...] - theta * band_theta + 8,
        theta_frac_ref[...],
        lax.broadcasted_iota(jnp.int32, (band_theta + 16, theta_start_ref.shape[1]), 0),
    )
    rows = split_dot(polar_weights, stacked, 0)

    band_phi = LANES // group
    lane = lax.broadcasted_iota(jnp.int32, (rows.shape[0], LANES), 1)
    own = 4 * group
    per_pack = LANES // own
    plane = [rows[:, j * LANES : (j + 1) * LANES] for j in range(len(planes))]
    for pack in range(len(planes) // per_pack):
        packed = jnp.zeros_like(plane[0])
        for j in range(per_pack):
            for g in range(group):
                at = own * j + 4 * g
                shift = (at - (g * band_phi - 2)) % LANES
                value = plane[pack * per_pack + j]
                value = pltpu.roll(value, shift, 1) if shift else value
                packed = jnp.where((lane >= at) & (lane < at + 4), value, packed)
        edges[pack] = packed
    to_right = send(edges, edge_left, edge_sem.at[0], right)
    to_left = send(edges, edge_right, edge_sem.at[1], left)
    to_right.start()
    to_left.start()

    width = phi_start_ref.shape[1]
    local_start = phi_start_ref[...] - phi * band_phi
    row = lax.broadcasted_iota(jnp.int32, (LANES, width), 0)
    own_group, own_node = row // band_phi, lax.rem(row, band_phi)
    slot = lax.rem(row, own) // 4
    offset = lax.rem(row, 4)
    from_left = (row < own) & (offset < 2)
    from_right = (row >= own) & (row < 2 * own) & (offset >= 2)
    edge_group = jnp.where(from_left, lax.rem(slot + group - 1, group), slot)
    edge_node = jnp.where(from_left, offset - 2, band_phi + offset - 2)
    own_taps = tap_weights(local_start, phi_frac_ref[...], own_node)
    edge_taps = tap_weights(local_start, phi_frac_ref[...], edge_node)
    edge_taps = jnp.where(from_left | from_right, edge_taps, 0.0)
    for g in range(group):
        columns = slice(g * width, (g + 1) * width)
        weights_ref[:LANES, columns] = jnp.where(own_group == g, own_taps, 0.0)
        weights_ref[LANES:, columns] = jnp.where(edge_group == g, edge_taps, 0.0)

    to_right.wait_recv()
    to_left.wait_recv()
    operand = []
    for j in range(len(planes)):
        pack, place = j // per_pack, j % per_pack
        from_l, from_r = edge_left[pack], edge_right[pack]
        shift_l, shift_r = (-own * place) % LANES, (own - own * place) % LANES
        from_l = pltpu.roll(from_l, shift_l, 1) if shift_l else from_l
        from_r = pltpu.roll(from_r, shift_r, 1) if shift_r else from_r
        operand.append(jnp.concatenate([plane[j], jnp.where(lane < own, from_l, from_r)], axis=1))
    field = split_dot(jnp.concatenate(operand, axis=0), weights_ref[...])
    incidences = out_ref.shape[0]
    height = rows.shape[0]
    power = [None] * incidences
    for j in range(len(planes)):
        for g in range(group):
            value = field[j * height : (j + 1) * height, g * width : (g + 1) * width]
            at = (g * units + j % units) % incidences
            power[at] = value * value if power[at] is None else power[at] + value * value
    for at in range(incidences):
        out_ref[at] = power[at]

    to_right.wait_send()
    to_left.wait_send()

    @pl.when(theta < count_theta - 1)
    def _():
        for k in range(chunks):
            row_to_after(k).wait_send()

    @pl.when(theta > 0)
    def _():
        for k in range(chunks):
            row_to_before(k).wait_send()

    @pl.loop(0, chunks // 2)
    def _(pair):
        for parity in range(2):
            k = pair * 2 + parity
            copies = core_copies(k) + first_copies(k, parity) + second_copies(k, parity)
            for copy in copies + far_copies(k):
                copy.wait_send()


def power_sum(
    pattern, up_phi, up_theta, offsets, rows_out, columns_out, count_phi, count_theta
):
    held, parts, group, units, polar, azimuth = pattern.shape
    rows, columns = direction_tables(group, count_phi)
    band_theta = NT // count_theta
    n_high, n_far = count_phi // 2, count_theta // 2
    chunks = min(CHUNKS, units)
    per_chunk = units // chunks
    tile = (parts, per_chunk, band_theta, LANES)
    whole = pl.BlockSpec(memory_space=pltpu.VMEM)
    peers = max(1, n_high - 1)
    height, width = rows_out[0].shape[0], columns_out[0].shape[0]
    channels = group * units
    packs = parts * channels * 4 // LANES
    return pl.pallas_call(
        root_kernel,
        out_shape=jax.ShapeDtypeStruct((channels // 2, height, width), jnp.float32),
        in_specs=[
            pl.BlockSpec(memory_space=pl.ANY), whole, whole,
            pl.BlockSpec(memory_space=pltpu.SMEM), whole, whole, whole, whole, whole, whole,
        ],
        out_specs=whole,
        scratch_shapes=[
            pltpu.VMEM((chunks, held, parts, group, per_chunk, polar, azimuth), jnp.bfloat16),
            pltpu.VMEM((group * azimuth, count_phi * LANES), jnp.bfloat16),
            pltpu.VMEM((NT, polar), jnp.bfloat16),
            pltpu.VMEM((held, NT, count_phi * LANES), jnp.float32),
            pltpu.VMEM((held, NT, count_phi * LANES), jnp.float32),
            pltpu.VMEM((held * parts * polar, count_phi * LANES), jnp.bfloat16),
            pltpu.VMEM((chunks, 2, n_high, 2, n_far) + tile, jnp.float32),
            pltpu.VMEM((chunks, n_high, 2, n_far) + tile, jnp.float32),
            pltpu.VMEM((chunks // 2, n_high, n_far) + tile, jnp.float32),
            pltpu.VMEM((chunks // 2, peers, 2, n_far) + tile, jnp.float32),
            pltpu.VMEM((chunks // 2, peers, n_far) + tile, jnp.float32),
            pltpu.VMEM((chunks // 2, n_far) + tile, jnp.float32),
            pltpu.VMEM((chunks, n_far - 1) + tile, jnp.float32),
            pltpu.VMEM((chunks,) + tile, jnp.float32),
            pltpu.VMEM((chunks, parts, per_chunk, 8, LANES), jnp.float32),
            pltpu.VMEM((chunks, parts, per_chunk, 8, LANES), jnp.float32),
            pltpu.VMEM((packs, height, LANES), jnp.float32),
            pltpu.VMEM((packs, height, LANES), jnp.float32),
            pltpu.VMEM((packs, height, LANES), jnp.float32),
            pltpu.VMEM((2 * LANES, group * width), jnp.float32),
            pltpu.SemaphoreType.DMA((chunks,)),
            pltpu.SemaphoreType.DMA((chunks, 2)),
            pltpu.SemaphoreType.DMA((chunks, peers, 2)),
            pltpu.SemaphoreType.DMA((chunks, peers, 2)),
            pltpu.SemaphoreType.DMA((chunks, n_far - 1, 2)),
            pltpu.SemaphoreType.DMA((chunks, 2, 2)),
            pltpu.SemaphoreType.DMA((2, 2)),
        ],
        compiler_params=pltpu.CompilerParams(
            vmem_limit_bytes=60 << 20, collective_id=0, has_side_effects=True
        ),
    )(
        pattern, up_phi, up_theta.T, offsets, jnp.asarray(rows), jnp.asarray(columns),
        *(value[None, :] for value in rows_out + columns_out),
    )


def per_device(
    subtree_pattern, up_phi, up_theta, offsets, theta_start, theta_frac, phi_start, phi_frac
):
    count_phi = lax.axis_size("phi")
    count_theta = lax.axis_size("theta")
    group = LANES * count_phi // NP
    held, parts, channels, polar, azimuth = subtree_pattern.shape
    units = channels // group
    pattern = subtree_pattern.reshape(held, parts, group, units, polar, azimuth)
    power = power_sum(
        pattern, up_phi, up_theta, offsets,
        (theta_start, theta_frac), (phi_start, phi_frac), count_phi, count_theta,
    )
    return power / (held * count_phi * count_theta)


def solution(mesh):
    return jax.shard_map(
        per_device,
        mesh=mesh,
        in_specs=(
            P(("phi", "theta"), None, None, None, None),
            P(),
            P(),
            P(None, ("phi", "theta")),
            P("theta"),
            P("theta"),
            P("phi"),
            P("phi"),
        ),
        out_specs=P(None, "theta", "phi"),
        check_vma=False,
    )
```

```python
import math

import jax
import jax.numpy as jnp
import numpy as np
from jax import lax
from jax.experimental import pallas as pl
from jax.experimental.pallas import tpu as pltpu
from jax.sharding import PartitionSpec as P

NT = 128
NP = 256
LANES = 128
CHUNKS = 16
FIRST_LAG = 4
SECOND_LAG = 8


def direction_tables(group, bands):
    polar = (np.arange(NT) + 0.5) * (math.pi / NT)
    rows = np.stack([np.sin(polar), np.cos(polar)])[:, :, None]
    rows = np.broadcast_to(rows, (2, NT, LANES))
    azimuth = (np.arange(NP) * (2.0 * math.pi / NP)).reshape(bands, 1, -1)
    azimuth = np.broadcast_to(azimuth, (bands, group, azimuth.shape[2])).reshape(1, -1)
    columns = np.stack([np.cos(azimuth), np.sin(azimuth)])
    columns = np.broadcast_to(columns, (2, 8, columns.shape[2]))
    return rows.astype(np.float32), columns.astype(np.float32)


def group_up_phi(source_ref, target_ref, group, bands):
    depth, band = source_ref.shape[0], NP // bands
    lane = lax.broadcasted_iota(jnp.int32, (depth, LANES), 1)
    for a in range(bands):
        tile, inside = divmod(a * band, LANES)
        columns = source_ref[:, tile * LANES : (tile + 1) * LANES].astype(jnp.float32)
        for g in range(group):
            shift = (g * band - inside) % LANES
            value = pltpu.roll(columns, shift, 1) if shift else columns
            value = jnp.where((lane >= g * band) & (lane < (g + 1) * band), value, 0.0)
            target_ref[g * depth : (g + 1) * depth, a * LANES : (a + 1) * LANES] = value.astype(
                jnp.bfloat16
            )


def turn_series():
    two_pi = 2.0 * math.pi
    sine = [(-1) ** k * two_pi ** (2 * k + 1) / math.factorial(2 * k + 1) for k in range(9)]
    cosine = [(-1) ** k * two_pi ** (2 * k) / math.factorial(2 * k) for k in range(10)]
    return sine, cosine


def horner(square, terms):
    value = jnp.full_like(square, terms[-1])
    for term in terms[-2::-1]:
        value = value * square + term
    return value


def phase_factors(offsets_ref, row_ref, column_ref, cos_ref, sin_ref):
    sine_terms, cosine_terms = turn_series()
    lane_groups = cos_ref.shape[2] // LANES

    @pl.loop(0, cos_ref.shape[0])
    def _(s):
        off_x, off_y, off_z = (offsets_ref[k, s] for k in range(3))
        for lane in range(lane_groups):
            lanes = slice(lane * LANES, (lane + 1) * LANES)
            wave = off_x * column_ref[0, 0:1, lanes] + off_y * column_ref[1, 0:1, lanes]
            turns = wave * row_ref[0] + off_z * row_ref[1]
            turns = turns - jnp.floor(turns + 0.5)
            square = turns * turns
            cos_ref[s, :, lanes] = horner(square, cosine_terms)
            sin_ref[s, :, lanes] = horner(square, sine_terms) * turns


def subtree_sum(pattern, phi_ref, theta_ref, coarse_ref, cos_ref, sin_ref, store):
    count, polar = cos_ref.shape[0], theta_ref.shape[1]
    parts = coarse_ref.shape[0] // (count * polar)
    rows = [pattern(s, r) for s in range(count) for r in range(parts)]
    coarse_ref[...] = jnp.dot(
        jnp.concatenate(rows, axis=0), phi_ref[...], preferred_element_type=jnp.float32
    ).astype(jnp.bfloat16)
    width = 2 * LANES
    for start in range(0, phi_ref.shape[1], width):
        lanes = slice(start, start + width)
        real_sum, imag_sum = None, None
        for s in range(count):
            real, imag = (
                jnp.dot(
                    theta_ref[...],
                    coarse_ref[(s * parts + r) * polar : (s * parts + r + 1) * polar, lanes],
                    preferred_element_type=jnp.float32,
                )
                for r in range(parts)
            )
            cosine, sine = cos_ref[s, :, lanes], sin_ref[s, :, lanes]
            real_part = real * cosine - imag * sine
            imag_part = real * sine + imag * cosine
            real_sum = real_part if s == 0 else real_sum + real_part
            imag_sum = imag_part if s == 0 else imag_sum + imag_part
        for k in range(width // LANES):
            piece = slice(k * LANES, (k + 1) * LANES)
            store(start // LANES + k, 0, real_sum[:, piece])
            store(start // LANES + k, 1, imag_sum[:, piece])


def tap_weights(start, frac, node):
    position = 1.0 + frac
    weights = [
        -(position - 1.0) * (position - 2.0) * (position - 3.0) / 6.0,
        position * (position - 2.0) * (position - 3.0) / 2.0,
        -position * (position - 1.0) * (position - 3.0) / 2.0,
        position * (position - 1.0) * (position - 2.0) / 6.0,
    ]
    matrix = jnp.zeros(node.shape, jnp.float32)
    for tap in range(4):
        matrix = matrix + jnp.where(node == start + tap, weights[tap], 0.0)
    return matrix


def split_dot(a, b, a_depth=1):
    a_high, b_high = a.astype(jnp.bfloat16), b.astype(jnp.bfloat16)
    a_low = (a - a_high.astype(jnp.float32)).astype(jnp.bfloat16)
    b_low = (b - b_high.astype(jnp.float32)).astype(jnp.bfloat16)

    def dot(left, right):
        numbers = (((a_depth,), (0,)), ((), ()))
        return lax.dot_general(left, right, numbers, preferred_element_type=jnp.float32)

    return dot(a_high, b_high) + (dot(a_high, b_low) + dot(a_low, b_high))


def root_kernel(
    pattern_hbm, up_phi_ref, up_theta_ref, offsets_ref, row_ref, column_ref,
    theta_start_ref, theta_frac_ref, phi_start_ref, phi_frac_ref, out_ref,
    pattern_ref, phi_ref, theta_ref, cos_ref, sin_ref, coarse_ref, sums,
    core_in, low_first, high_first, high_second, low_second, far_in,
    root, row_low, row_high, edges, edge_left, edge_right, weights_ref,
    load_sem, core_sem, first_sem, second_sem, far_sem, row_sem, edge_sem,
):
    chunks, _, n_high, _, n_far, parts, per_chunk, band_theta, _ = sums.shape
    group = pattern_ref.shape[3]
    phi, theta = lax.axis_index("phi"), lax.axis_index("theta")
    high, low = phi // 2, lax.rem(phi, 2)
    far, core = theta // 2, lax.rem(theta, 2)

    def turned(index, step, count):
        return lax.rem(index + step, count)

    core_peer = (phi, far * 2 + 1 - core)
    low_peer = (high * 2 + 1 - low, theta)

    def high_peer(step):
        return (turned(high, step, n_high) * 2 + low, theta)

    def far_peer(step):
        return (phi, turned(far, step, n_far) * 2 + core)

    def send(source, target, sems, peer):
        return pltpu.make_async_remote_copy(
            src_ref=source,
            dst_ref=target,
            send_sem=sems.at[0],
            recv_sem=sems.at[1],
            device_id=peer,
            device_id_type=pl.DeviceIdType.MESH,
        )

    def core_copies(k):
        return [send(sums.at[k, 1 - core], core_in.at[k], core_sem.at[k], core_peer)]

    def first_copies(k, parity):
        if parity == 0:
            source = sums.at[k, core, :, 1 - low]
            return [send(source, low_first.at[k // 2], first_sem.at[k, 0], low_peer)]
        return [
            send(
                sums.at[k, core, turned(high, d, n_high)],
                high_first.at[k // 2, d - 1],
                first_sem.at[k, d - 1],
                high_peer(d),
            )
            for d in range(1, n_high)
        ]

    def second_copies(k, parity):
        if parity == 1:
            source = sums.at[k, core, high, 1 - low]
            return [send(source, low_second.at[k // 2], second_sem.at[k, 0], low_peer)]
        return [
            send(
                sums.at[k, core, turned(high, d, n_high), low],
                high_second.at[k // 2, d - 1],
                second_sem.at[k, d - 1],
                high_peer(d),
            )
            for d in range(1, n_high)
        ]

    def far_copies(k):
        return [
            send(
                sums.at[k, core, high, low, turned(far, d, n_far)],
                far_in.at[k, d - 1],
                far_sem.at[k, d - 1],
                far_peer(d),
            )
            for d in range(1, n_far)
        ]

    count_phi, count_theta = n_high * 2, n_far * 2
    before = (phi, lax.rem(theta + count_theta - 1, count_theta))
    after = (phi, lax.rem(theta + 1, count_theta))
    left = (lax.rem(phi + count_phi - 1, count_phi), theta)
    right = (lax.rem(phi + 1, count_phi), theta)

    def row_to_after(k):
        return send(
            root.at[k, :, :, pl.ds(band_theta - 8, 8)], row_low.at[k], row_sem.at[k, 0], after
        )

    def row_to_before(k):
        return send(root.at[k, :, :, pl.ds(0, 8)], row_high.at[k], row_sem.at[k, 1], before)

    def start(copies):
        for copy in copies:
            copy.start()

    def arrive(copies):
        for copy in copies:
            copy.wait_recv()

    def after_core(k, parity):
        arrive(core_copies(k))
        sums[k, core] = sums[k, core] + core_in[k]
        start(first_copies(k, parity))

    def after_first(k, parity):
        arrive(first_copies(k, parity))
        if parity == 0:
            for h in range(n_high):
                sums[k, core, h, low] = sums[k, core, h, low] + low_first[k // 2, h]
        else:
            total = sums[k, core, high]
            for d in range(1, n_high):
                total = total + high_first[k // 2, d - 1]
            sums[k, core, high] = total
        start(second_copies(k, parity))

    def after_second(k, parity):
        arrive(second_copies(k, parity))
        total = sums[k, core, high, low]
        if parity == 1:
            total = total + low_second[k // 2]
        else:
            for d in range(1, n_high):
                total = total + high_second[k // 2, d - 1]
        sums[k, core, high, low] = total
        start(far_copies(k))

    def load(k):
        return pltpu.make_async_copy(
            pattern_hbm.at[:, :, :, pl.ds(k * per_chunk, per_chunk)],
            pattern_ref.at[k],
            load_sem.at[k],
        )

    for k in range(chunks):
        load(k).start()

    peers = [core_peer, low_peer]
    peers += [high_peer(d) for d in range(1, n_high)] + [far_peer(d) for d in range(1, n_far)]
    peers += [before, after, left, right]
    barrier = pltpu.get_barrier_semaphore()
    for peer in peers:
        pl.semaphore_signal(barrier, inc=1, device_id=peer, device_id_type=pl.DeviceIdType.MESH)
    group_up_phi(up_phi_ref, phi_ref, group, n_high * 2)
    theta_ref[...] = up_theta_ref[...].astype(jnp.float32).T.astype(jnp.bfloat16)
    phase_factors(offsets_ref, row_ref, column_ref, cos_ref, sin_ref)
    pl.semaphore_wait(barrier, len(peers))

    def compute(k):
        load(k).wait()

        @pl.loop(0, per_chunk)
        def _(unit):
            def pattern(s, r):
                return jnp.concatenate(
                    [pattern_ref[k, s, r, g, unit] for g in range(group)], axis=1
                )

            def store(band, part, value):
                value = value.reshape(n_far, 2, band_theta, LANES)
                for c in range(2):
                    sums[k, c, band // 2, band % 2, :, part, unit] = value[:, c]

            subtree_sum(pattern, phi_ref, theta_ref, coarse_ref, cos_ref, sin_ref, store)

    stages = ((1, after_core), (FIRST_LAG, after_first), (SECOND_LAG, after_second))

    @pl.loop(0, chunks // 2)
    def _(pair):
        for parity in range(2):
            k = pair * 2 + parity
            compute(k)
            start(core_copies(k))
            for lag, stage in stages:

                @pl.when(k >= lag)
                def _(lag=lag, stage=stage, k=k, parity=parity):
                    stage(k - lag, (parity - lag) % 2)

    for step in range(chunks, chunks + SECOND_LAG):
        for lag, stage in stages:
            if step - lag < chunks:
                stage(step - lag, (step - lag) % 2)

    for k in range(chunks):
        arrive(far_copies(k))
        total = sums[k, core, high, low, far]
        for d in range(1, n_far):
            total = total + far_in[k, d - 1]
        root[k] = total

        @pl.when(theta < count_theta - 1)
        def _(k=k):
            row_to_after(k).start()

        @pl.when(theta > 0)
        def _(k=k):
            row_to_before(k).start()

    @pl.when(theta > 0)
    def _():
        for k in range(chunks):
            row_to_after(k).wait_recv()

    @pl.when(theta == 0)
    def _():
        row_low[...] = jnp.zeros_like(row_low)

    @pl.when(theta < count_theta - 1)
    def _():
        for k in range(chunks):
            row_to_before(k).wait_recv()

    @pl.when(theta == count_theta - 1)
    def _():
        row_high[...] = jnp.zeros_like(row_high)

    units = chunks * per_chunk
    planes = [(r, k, u) for r in range(parts) for k in range(chunks) for u in range(per_chunk)]
    stacked = jnp.concatenate(
        [
            jnp.concatenate([row_low[k, r, u], root[k, r, u], row_high[k, r, u]], axis=0)
            for r, k, u in planes
        ],
        axis=1,
    )
    polar_weights = tap_weights(
        theta_start_ref[...] - theta * band_theta + 8,
        theta_frac_ref[...],
        lax.broadcasted_iota(jnp.int32, (band_theta + 16, theta_start_ref.shape[1]), 0),
    )
    rows = split_dot(polar_weights, stacked, 0)

    band_phi = LANES // group
    lane = lax.broadcasted_iota(jnp.int32, (rows.shape[0], LANES), 1)
    own = 4 * group
    per_pack = LANES // own
    plane = [rows[:, j * LANES : (j + 1) * LANES] for j in range(len(planes))]
    for pack in range(len(planes) // per_pack):
        packed = jnp.zeros_like(plane[0])
        for j in range(per_pack):
            for g in range(group):
                at = own * j + 4 * g
                shift = (at - (g * band_phi - 2)) % LANES
                value = plane[pack * per_pack + j]
                value = pltpu.roll(value, shift, 1) if shift else value
                packed = jnp.where((lane >= at) & (lane < at + 4), value, packed)
        edges[pack] = packed
    to_right = send(edges, edge_left, edge_sem.at[0], right)
    to_left = send(edges, edge_right, edge_sem.at[1], left)
    to_right.start()
    to_left.start()

    width = phi_start_ref.shape[1]
    local_start = phi_start_ref[...] - phi * band_phi
    row = lax.broadcasted_iota(jnp.int32, (LANES, width), 0)
    own_group, own_node = row // band_phi, lax.rem(row, band_phi)
    slot = lax.rem(row, own) // 4
    offset = lax.rem(row, 4)
    from_left = (row < own) & (offset < 2)
    from_right = (row >= own) & (row < 2 * own) & (offset >= 2)
    edge_group = jnp.where(from_left, lax.rem(slot + group - 1, group), slot)
    edge_node = jnp.where(from_left, offset - 2, band_phi + offset - 2)
    own_taps = tap_weights(local_start, phi_frac_ref[...], own_node)
    edge_taps = tap_weights(local_start, phi_frac_ref[...], edge_node)
    edge_taps = jnp.where(from_left | from_right, edge_taps, 0.0)
    for g in range(group):
        columns = slice(g * width, (g + 1) * width)
        weights_ref[:LANES, columns] = jnp.where(own_group == g, own_taps, 0.0)
        weights_ref[LANES:, columns] = jnp.where(edge_group == g, edge_taps, 0.0)

    to_right.wait_recv()
    to_left.wait_recv()
    operand = []
    for j in range(len(planes)):
        pack, place = j // per_pack, j % per_pack
        from_l, from_r = edge_left[pack], edge_right[pack]
        shift_l, shift_r = (-own * place) % LANES, (own - own * place) % LANES
        from_l = pltpu.roll(from_l, shift_l, 1) if shift_l else from_l
        from_r = pltpu.roll(from_r, shift_r, 1) if shift_r else from_r
        operand.append(jnp.concatenate([plane[j], jnp.where(lane < own, from_l, from_r)], axis=1))
    field = split_dot(jnp.concatenate(operand, axis=0), weights_ref[...])
    incidences = out_ref.shape[0]
    subtrees = cos_ref.shape[0] * count_phi * count_theta
    height = rows.shape[0]
    power = [None] * incidences
    for j in range(len(planes)):
        for g in range(group):
            value = field[j * height : (j + 1) * height, g * width : (g + 1) * width]
            at = (g * units + j % units) % incidences
            power[at] = value * value if power[at] is None else power[at] + value * value
    for at in range(incidences):
        out_ref[at] = power[at] * (1.0 / subtrees)

    to_right.wait_send()
    to_left.wait_send()

    @pl.when(theta < count_theta - 1)
    def _():
        for k in range(chunks):
            row_to_after(k).wait_send()

    @pl.when(theta > 0)
    def _():
        for k in range(chunks):
            row_to_before(k).wait_send()

    @pl.loop(0, chunks // 2)
    def _(pair):
        for parity in range(2):
            k = pair * 2 + parity
            copies = core_copies(k) + first_copies(k, parity) + second_copies(k, parity)
            for copy in copies + far_copies(k):
                copy.wait_send()


def power_sum(
    pattern, up_phi, up_theta, offsets, rows_out, columns_out, count_phi, count_theta
):
    held, parts, group, units, polar, azimuth = pattern.shape
    rows, columns = direction_tables(group, count_phi)
    band_theta = NT // count_theta
    n_high, n_far = count_phi // 2, count_theta // 2
    chunks = min(CHUNKS, units)
    per_chunk = units // chunks
    tile = (parts, per_chunk, band_theta, LANES)
    whole = pl.BlockSpec(memory_space=pltpu.VMEM)
    peers = max(1, n_high - 1)
    height, width = rows_out[0].shape[0], columns_out[0].shape[0]
    channels = group * units
    packs = parts * channels * 4 // LANES
    return pl.pallas_call(
        root_kernel,
        out_shape=jax.ShapeDtypeStruct((channels // 2, height, width), jnp.float32),
        in_specs=[
            pl.BlockSpec(memory_space=pl.ANY), whole, whole,
            pl.BlockSpec(memory_space=pltpu.SMEM), whole, whole, whole, whole, whole, whole,
        ],
        out_specs=whole,
        scratch_shapes=[
            pltpu.VMEM((chunks, held, parts, group, per_chunk, polar, azimuth), jnp.bfloat16),
            pltpu.VMEM((group * azimuth, count_phi * LANES), jnp.bfloat16),
            pltpu.VMEM((NT, polar), jnp.bfloat16),
            pltpu.VMEM((held, NT, count_phi * LANES), jnp.float32),
            pltpu.VMEM((held, NT, count_phi * LANES), jnp.float32),
            pltpu.VMEM((held * parts * polar, count_phi * LANES), jnp.bfloat16),
            pltpu.VMEM((chunks, 2, n_high, 2, n_far) + tile, jnp.float32),
            pltpu.VMEM((chunks, n_high, 2, n_far) + tile, jnp.float32),
            pltpu.VMEM((chunks // 2, n_high, n_far) + tile, jnp.float32),
            pltpu.VMEM((chunks // 2, peers, 2, n_far) + tile, jnp.float32),
            pltpu.VMEM((chunks // 2, peers, n_far) + tile, jnp.float32),
            pltpu.VMEM((chunks // 2, n_far) + tile, jnp.float32),
            pltpu.VMEM((chunks, n_far - 1) + tile, jnp.float32),
            pltpu.VMEM((chunks,) + tile, jnp.float32),
            pltpu.VMEM((chunks, parts, per_chunk, 8, LANES), jnp.float32),
            pltpu.VMEM((chunks, parts, per_chunk, 8, LANES), jnp.float32),
            pltpu.VMEM((packs, height, LANES), jnp.float32),
            pltpu.VMEM((packs, height, LANES), jnp.float32),
            pltpu.VMEM((packs, height, LANES), jnp.float32),
            pltpu.VMEM((2 * LANES, group * width), jnp.float32),
            pltpu.SemaphoreType.DMA((chunks,)),
            pltpu.SemaphoreType.DMA((chunks, 2)),
            pltpu.SemaphoreType.DMA((chunks, peers, 2)),
            pltpu.SemaphoreType.DMA((chunks, peers, 2)),
            pltpu.SemaphoreType.DMA((chunks, n_far - 1, 2)),
            pltpu.SemaphoreType.DMA((chunks, 2, 2)),
            pltpu.SemaphoreType.DMA((2, 2)),
        ],
        compiler_params=pltpu.CompilerParams(
            vmem_limit_bytes=60 << 20, collective_id=0, has_side_effects=True
        ),
    )(
        pattern, up_phi, up_theta.T, offsets, jnp.asarray(rows), jnp.asarray(columns),
        *(value[None, :] for value in rows_out + columns_out),
    )


def per_device(
    subtree_pattern, up_phi, up_theta, offsets, theta_start, theta_frac, phi_start, phi_frac
):
    count_phi = lax.axis_size("phi")
    count_theta = lax.axis_size("theta")
    group = LANES * count_phi // NP
    held, parts, channels, polar, azimuth = subtree_pattern.shape
    units = channels // group
    pattern = subtree_pattern.reshape(held, parts, group, units, polar, azimuth)
    return power_sum(
        pattern, up_phi, up_theta, offsets,
        (theta_start, theta_frac), (phi_start, phi_frac), count_phi, count_theta,
    )


def solution(mesh):
    return jax.shard_map(
        per_device,
        mesh=mesh,
        in_specs=(
            P(("phi", "theta"), None, None, None, None),
            P(),
            P(),
            P(None, ("phi", "theta")),
            P("theta"),
            P("theta"),
            P("phi"),
            P("phi"),
        ),
        out_specs=P(None, "theta", "phi"),
        check_vma=False,
    )
```
